512 devices in a mesh: row: 4 (over x), col: 16 (over z_lo, y), depth: 8 (over z_hi, core).
Axes of the slice: x: 4, y: 4, z: 16 (z_hi: 4, z_lo: 4; z = z_hi * 4 + z_lo), core: 2. Of those that a mesh axis runs over, the one named last changes fastest.
Arguments:
- amplitude: float32 [100, 512, 2048], P('row', 'depth', 'col'), may hold values from -6 to 6
- integral: float32 [512, 100, 8192], P('depth', None, 'col'), may hold values from -0.02734375 to 0.02734375
Outputs:
- cycle_term: float32 [2048, 8192], P(('row', 'depth'), 'col')
The draws below stay inside these ranges and needn't reach their ends.
All inputs are finite; a program needn't handle non-finite values.
Results may differ from the reference program's by a relative error of at most 0.00011.
Values sent between devices are 32-bit elements; how exact they have to be, the bound alone decides.
A program may use at most 128 MiB of HBM per device.

```python
import jax
import jax.numpy as jnp
from jax import lax

O = 100
VC = 512
ROWS = 2048
COLS = 8192


def levels(stream_key, extent, split, low, high):
    factor_of = 1.0
    for position, blocks in split:
        draws = jax.random.uniform(jax.random.fold_in(jax.random.fold_in(stream_key, 6), position), (blocks,), jnp.float32, low / len(split), high / len(split))
        factor_of = factor_of * jnp.repeat(jnp.exp(draws), extent[position] // blocks).reshape((-1,) + (1,) * (len(extent) - 1 - position))
    return factor_of


def scatter_about(key, shape, width, reach, cuts=(), kind=jnp.bfloat16):
    level = levels(key, shape, cuts, -0.22, 0.18) if cuts else 1.0
    entries = jax.random.normal(key, shape, jnp.float32) * width * level
    return jnp.minimum(jnp.maximum(entries, -reach), reach).astype(kind)


def setup_inputs(seed: int = 0) -> dict:
    seeds = jax.random.split(jax.random.key(seed), 3)
    amplitude = scatter_about(seeds[0], (O, VC, ROWS), 1.0, 6.0, ((0, 4), (1, 8), (2, 16)), jnp.float32)
    integral = scatter_about(seeds[1], (VC, O, COLS), (VC * O) ** -0.5, 0.02734375, ((0, 8), (2, 16)), jnp.float32)
    return dict(amplitude=amplitude, integral=integral)


def reference(amplitude, integral):
    return jnp.einsum("kcm,ckn->mn", amplitude, integral, precision=lax.Precision.HIGHEST, preferred_element_type=jnp.float32)
```

```python
import functools

import jax
import jax.numpy as jnp
from jax import lax
from jax.experimental import pallas as pl
from jax.experimental.pallas import tpu as pltpu
from jax.sharding import PartitionSpec as P

MESH = pl.DeviceIdType.MESH
CH = 5
KC = 5
AHEAD = 3


def order(z, p):
    hi = z // 2
    zz = z + hi * (3 - 2 * z)
    base = p + zz * (1 - 2 * p) if p < 2 else p
    return base + hi * (3 - 2 * base)


def kernel(
    amp, integ, out,
    abuf, at_h, at_l, bown, bh, bl, ib, part, r1, r2, r3, fin,
    loc, zr, zd, zu, yr, ys, ir, js, s1s, s1r, s2s, s2r, s3s, s3r, s4s, s4r,
):
    x = lax.axis_index("row")
    col = lax.axis_index("col")
    dep = lax.axis_index("depth")
    z, y = col // 4, lax.rem(col, 4)
    h, core = dep // 2, lax.rem(dep, 2)
    yp = 3 - y
    yq = y + 1 - 2 * lax.rem(y, 2)
    ords = [order(z, p) for p in range(4)]

    def dev(x_=None, y_=None, z_=None, h_=None, core_=None):
        return (
            x if x_ is None else x_,
            (z if z_ is None else z_) * 4 + (y if y_ is None else y_),
            (h if h_ is None else h_) * 2 + (core if core_ is None else core_),
        )

    def remote(src, dst, ss, rs, to):
        return pltpu.make_async_remote_copy(
            src_ref=src, dst_ref=dst, send_sem=ss, recv_sem=rs,
            device_id=to, device_id_type=MESH,
        )

    own_a = pltpu.make_async_copy(amp, abuf.at[z], loc.at[0])
    own_b = pltpu.make_async_copy(integ.at[pl.ds(25 * x, 25)], bown, loc.at[1])
    own_a.start()
    own_b.start()

    barrier = pltpu.get_barrier_semaphore()

    def greet(to):
        pl.semaphore_signal(barrier, inc=1, device_id=to, device_id_type=MESH)

    greet(dev(y_=yp))
    greet(dev(y_=yq))
    greet(dev(core_=1 - core))
    for i in range(1, 4):
        greet(dev(x_=lax.rem(x + i, 4)))
        greet(dev(h_=lax.rem(h + i, 4)))

    @pl.when(z > 0)
    def _():
        greet(dev(z_=z - 1))

    @pl.when(z < 3)
    def _():
        greet(dev(z_=z + 1))

    @pl.when((z > 0) & (z < 3))
    def _():
        pl.semaphore_wait(barrier, 11)

    @pl.when((z == 0) | (z == 3))
    def _():
        pl.semaphore_wait(barrier, 10)

    own_a.wait()

    def int_copy(p, c):
        return remote(
            integ.at[pl.ds(25 * x + KC * c, KC), :, pl.ds(128 * p, 128)],
            ib.at[p, pl.ds(KC * c, KC)],
            js.at[p, c], ir.at[p, c], dev(y_=yq),
        )

    def y_copy(p, c):
        a = ords[p]
        ks = pl.ds(KC * c, KC)
        return remote(abuf.at[a, ks], abuf.at[4 + a, ks], ys.at[a, c], yr.at[a, c], dev(y_=yp))

    def z_copy(a, c, to, sem):
        ks = pl.ds(KC * c, KC)
        return remote(abuf.at[a, ks], abuf.at[a, ks], sem.at[a, c], zr.at[a, c], dev(z_=to))

    def feed(p, c, do_z):
        int_copy(p, c).start()
        y_copy(p, c).start()
        if p < 3:
            @pl.when((z > 0) & (z + p <= 3))
            def _():
                z_copy(z + p, c, z - 1, zd).start()

            @pl.when((z < 3) & (z - p >= 0))
            def _():
                z_copy(z - p, c, z + 1, zu).start()

    def arrive(p, c):
        int_copy(p, c).wait_recv()
        y_copy(p, c).wait_recv()
        if p < 3:
            @pl.when(z + p + 1 <= 3)
            def _():
                z_copy(z + p + 1, c, z - 1, zd).wait_recv()

            @pl.when(z - p - 1 >= 0)
            def _():
                z_copy(z - p - 1, c, z + 1, zu).wait_recv()

    def tick(t):
        arrive(t // CH, t % CH)
        if t + AHEAD < 4 * CH:
            feed((t + AHEAD) // CH, (t + AHEAD) % CH, True)

    def messages(p):
        got = []
        if p <= 3:
            got.append((0, p, True))
        if p >= 1:
            got.append((1, p - 1, True))
        for e in range(min(p, 4)):
            got.append((0, e, False))
        for e in range(p - 1):
            got.append((1, e, False))
        return got

    def cols_of(p, new):
        return (0, 512 + 128 * p) if new else (512 + 128 * (p - 1), 128)

    def slot_of(side, e):
        return 4 * side + ords[e]

    def split(v):
        hi = v.astype(jnp.bfloat16)
        return hi, (v - hi.astype(jnp.float32)).astype(jnp.bfloat16)

    def prep_a(slot):
        t = abuf[slot].reshape(1600, 128).T
        hi, lo = split(t)
        at_h[slot] = hi
        at_l[slot] = lo

    def multiply(slot, c0, width):
        ah = at_h[slot]
        al = at_l[slot]
        n0 = c0
        while n0 < c0 + width:
            w = min(256, c0 + width - n0)
            b_h = bh[:, n0:n0 + w]
            b_l = bl[:, n0:n0 + w]
            acc = jnp.dot(ah, b_l, preferred_element_type=jnp.float32)
            acc += jnp.dot(al, b_h, preferred_element_type=jnp.float32)
            acc += jnp.dot(ah, b_h, preferred_element_type=jnp.float32)
            part[slot, :, :, n0:n0 + w] = acc.reshape(2, 64, w)
            n0 += w

    def s1_copy(p, m):
        side, e, new = m
        slot = slot_of(side, e)
        c0, w = cols_of(p, new)
        cs = pl.ds(c0, w)
        return remote(
            part.at[slot, 1 - core, :, cs], r1.at[slot, :, cs],
            s1s.at[slot, p], s1r.at[slot, p], dev(core_=1 - core),
        )

    def s2_copy(p, m, src_x):
        side, e, new = m
        slot = slot_of(side, e)
        c0, w = cols_of(p, new)
        cs = pl.ds(c0, w)
        a = ords[e]
        i = lax.rem(src_x - a + 3, 4)
        return remote(
            part.at[slot, core, :, cs], r2.at[side, i, :, cs],
            s2s.at[slot, p], s2r.at[side, i, p], dev(x_=a),
        )

    def s3_copy(p, m, src_h):
        side, e, new = m
        slot = slot_of(side, e)
        c0, w = cols_of(p, new)
        cs = pl.ds(c0, w)
        b = yp if side else y
        i = lax.rem(src_h - b + 3, 4)
        return remote(
            part.at[slot, core, :, cs], r3.at[i, :, cs],
            s3s.at[side, p], s3r.at[i, p], dev(h_=b),
        )

    def s4_copy(p, m):
        side, e, new = m
        slot = slot_of(side, e)
        c0, w = cols_of(p, new)
        if new:
            c0, w = 512, w - 512
        return remote(
            part.at[slot, core, :, pl.ds(c0, w)], fin.at[:, pl.ds(c0 - 512, w)],
            s4s.at[p], s4r.at[p], dev(y_=yq),
        )

    def stage2(p):
        for m in messages(p):
            side, e, new = m
            slot = slot_of(side, e)
            c0, w = cols_of(p, new)
            s1_copy(p, m).wait_recv()
            part[slot, core, :, c0:c0 + w] = part[slot, core, :, c0:c0 + w] + r1[slot, :, c0:c0 + w]

            @pl.when(ords[e] != x)
            def _():
                s2_copy(p, m, x).start()

    def stage3(p):
        for m in messages(p):
            side, e, new = m
            slot = slot_of(side, e)
            c0, w = cols_of(p, new)
            b = yp if side else y

            @pl.when(ords[e] == x)
            def _():
                for i in range(3):
                    s2_copy(p, m, lax.rem(ords[e] + 1 + i, 4)).wait_recv()
                part[slot, core, :, c0:c0 + w] = (
                    part[slot, core, :, c0:c0 + w] + r2[side, 0, :, c0:c0 + w]
                ) + (r2[side, 1, :, c0:c0 + w] + r2[side, 2, :, c0:c0 + w])

                @pl.when(h != b)
                def _():
                    s3_copy(p, m, h).start()

    def stage4(p):
        for m in messages(p):
            side, e, new = m
            slot = slot_of(side, e)
            c0, w = cols_of(p, new)
            b = yp if side else y

            @pl.when((ords[e] == x) & (h == b))
            def _():
                for i in range(3):
                    s3_copy(p, m, lax.rem(b + 1 + i, 4)).wait_recv()
                total = (part[slot, core, :, c0:c0 + w] + r3[0, :, c0:c0 + w]) + (
                    r3[1, :, c0:c0 + w] + r3[2, :, c0:c0 + w]
                )
                if new:
                    out[...] = total[:, :512]
                    if p:
                        part[slot, core, :, 512:c0 + w] = total[:, 512:]
                else:
                    part[slot, core, :, c0:c0 + w] = total
                if p:
                    s4_copy(p, m).start()

    def compute_new(p):
        for m in messages(p):
            if m[2]:
                slot = slot_of(m[0], m[1])
                prep_a(slot)
                multiply(slot, *cols_of(p, True))
                s1_copy(p, m).start()

    def compute_old(p):
        for m in messages(p):
            if not m[2]:
                multiply(slot_of(m[0], m[1]), *cols_of(p, False))
                s1_copy(p, m).start()

    def prep_b_own():
        @pl.loop(0, 25)
        def _(k):
            hi, lo = split(bown[k])
            rows = pl.ds(pl.multiple_of(64 * k, 64), 64)
            bh[rows, 0:512] = hi
            bl[rows, 0:512] = lo

    def prep_b(q):
        @pl.loop(0, 25)
        def _(k):
            hi, lo = split(ib[q, k])
            rows = pl.ds(pl.multiple_of(64 * k, 64), 64)
            bh[rows, 512 + 128 * q:640 + 128 * q] = hi
            bl[rows, 512 + 128 * q:640 + 128 * q] = lo

    for t in range(AHEAD):
        feed(t // CH, t % CH, True)
    own_b.wait()
    tick(0)
    prep_b_own()
    tick(1)
    compute_new(0)
    tick(2)
    tick(3)
    tick(4)
    for p in range(1, 4):
        tick(CH * p)
        prep_b(p - 1)
        stage2(p - 1)
        compute_new(p)
        tick(CH * p + 1)
        tick(CH * p + 2)
        compute_old(p)
        tick(CH * p + 3)
        stage3(p - 1)
        if p >= 2:
            stage4(p - 2)
        tick(CH * p + 4)
    prep_b(3)
    stage2(3)
    compute_new(4)
    compute_old(4)
    stage4(2)
    stage3(3)
    stage2(4)
    stage3(4)
    stage4(3)
    stage4(4)

    for side in range(2):
        b = 3 - yq if side else yq
        for e in range(4):
            @pl.when((ords[e] == x) & (h == b))
            def _():
                first = e + side
                for p in range(max(first, 1), 5):
                    s4_copy(p, (side, e, p == first)).wait_recv()
                out[...] = fin[...]

    for p in range(4):
        for c in range(CH):
            int_copy(p, c).wait_send()
            y_copy(p, c).wait_send()
            if p < 3:
                @pl.when((z > 0) & (z + p <= 3))
                def _():
                    z_copy(z + p, c, z - 1, zd).wait_send()

                @pl.when((z < 3) & (z - p >= 0))
                def _():
                    z_copy(z - p, c, z + 1, zu).wait_send()
    for p in range(5):
        for m in messages(p):
            side, e, new = m
            b = yp if side else y
            s1_copy(p, m).wait_send()

            @pl.when(ords[e] != x)
            def _():
                s2_copy(p, m, x).wait_send()

            @pl.when((ords[e] == x) & (h != b))
            def _():
                s3_copy(p, m, h).wait_send()

            if p:
                @pl.when((ords[e] == x) & (h == b))
                def _():
                    s4_copy(p, m).wait_send()


def shards(amplitude, integral):
    f32, bf16 = jnp.float32, jnp.bfloat16
    dma = pltpu.SemaphoreType.DMA
    return pl.pallas_call(
        kernel,
        out_shape=jax.ShapeDtypeStruct((64, 512), f32),
        in_specs=[pl.BlockSpec(memory_space=pl.ANY)] * 2,
        out_specs=pl.BlockSpec(memory_space=pltpu.VMEM),
        scratch_shapes=[
            pltpu.VMEM((8, 25, 64, 128), f32),
            pltpu.VMEM((8, 128, 1600), bf16),
            pltpu.VMEM((8, 128, 1600), bf16),
            pltpu.VMEM((25, 64, 512), f32),
            pltpu.VMEM((1600, 1024), bf16),
            pltpu.VMEM((1600, 1024), bf16),
            pltpu.VMEM((4, 25, 64, 128), f32),
            pltpu.VMEM((8, 2, 64, 1024), f32),
            pltpu.VMEM((8, 64, 1024), f32),
            pltpu.VMEM((2, 3, 64, 1024), f32),
            pltpu.VMEM((3, 64, 1024), f32),
            pltpu.VMEM((64, 512), f32),
            dma((2,)),
            dma((4, CH)), dma((4, CH)), dma((4, CH)),
            dma((4, CH)), dma((4, CH)),
            dma((4, CH)), dma((4, CH)),
            dma((8, 5)), dma((8, 5)),
            dma((8, 5)), dma((2, 3, 5)),
            dma((2, 5)), dma((3, 5)),
            dma((5,)), dma((5,)),
        ],
        compiler_params=pltpu.CompilerParams(
            collective_id=0, has_side_effects=True, vmem_limit_bytes=56 << 20
        ),
    )(amplitude, jnp.transpose(integral, (1, 0, 2)))


def solution(mesh):
    return jax.shard_map(
        shards,
        mesh=mesh,
        in_specs=(P("row", "depth", "col"), P("depth", None, "col")),
        out_specs=P(("row", "depth"), "col"),
        check_vma=False,
    )
```

```python
import functools

import jax
import jax.numpy as jnp
from jax import lax
from jax.experimental import pallas as pl
from jax.experimental.pallas import tpu as pltpu
from jax.sharding import PartitionSpec as P

MESH = pl.DeviceIdType.MESH
CH = 5
KC = 5
AHEAD = 3


def order(z, p):
    hi = z // 2
    zz = z + hi * (3 - 2 * z)
    base = p + zz * (1 - 2 * p) if p < 2 else p
    return base + hi * (3 - 2 * base)


def kernel(
    amp, integ, out,
    abuf, at_h, at_l, bown, bh, bl, ib, part, r1, r2, r3, fin,
    loc, zr, zd, zu, yr, ys, ir, js, s1s, s1r, s2s, s2r, s3s, s3r, s4s, s4r,
):
    x = lax.axis_index("row")
    col = lax.axis_index("col")
    dep = lax.axis_index("depth")
    z, y = col // 4, lax.rem(col, 4)
    h, core = dep // 2, lax.rem(dep, 2)
    yp = 3 - y

    def flip(v):
        return v + 1 - 2 * lax.rem(v, 2)

    yq = flip(y)
    ords = [order(z, p) for p in range(4)]

    def dev(x_=None, y_=None, z_=None, h_=None, core_=None):
        return (
            x if x_ is None else x_,
            (z if z_ is None else z_) * 4 + (y if y_ is None else y_),
            (h if h_ is None else h_) * 2 + (core if core_ is None else core_),
        )

    def remote(src, dst, ss, rs, to):
        return pltpu.make_async_remote_copy(
            src_ref=src, dst_ref=dst, send_sem=ss, recv_sem=rs,
            device_id=to, device_id_type=MESH,
        )

    own_a = pltpu.make_async_copy(amp, abuf.at[z], loc.at[0])
    own_b = pltpu.make_async_copy(integ.at[pl.ds(25 * x, 25)], bown, loc.at[1])
    own_a.start()
    own_b.start()

    barrier = pltpu.get_barrier_semaphore()

    def greet(to):
        pl.semaphore_signal(barrier, inc=1, device_id=to, device_id_type=MESH)

    greet(dev(y_=yp))
    greet(dev(y_=yq))
    greet(dev(core_=1 - core))
    for i in range(1, 4):
        greet(dev(x_=lax.rem(x + i, 4)))
        greet(dev(h_=lax.rem(h + i, 4)))

    @pl.when(z > 0)
    def _():
        greet(dev(z_=z - 1))

    @pl.when(z < 3)
    def _():
        greet(dev(z_=z + 1))

    @pl.when((z > 0) & (z < 3))
    def _():
        pl.semaphore_wait(barrier, 11)

    @pl.when((z == 0) | (z == 3))
    def _():
        pl.semaphore_wait(barrier, 10)

    own_a.wait()

    def int_copy(p, c):
        return remote(
            integ.at[pl.ds(25 * x + KC * c, KC), :, pl.ds(128 * p, 128)],
            ib.at[p, pl.ds(KC * c, KC)],
            js.at[p, c], ir.at[p, c], dev(y_=yq),
        )

    def y_copy(p, c):
        a = ords[p]
        ks = pl.ds(KC * c, KC)
        return remote(abuf.at[a, ks], abuf.at[4 + a, ks], ys.at[a, c], yr.at[a, c], dev(y_=yp))

    def z_copy(a, c, to, sem):
        ks = pl.ds(KC * c, KC)
        return remote(abuf.at[a, ks], abuf.at[a, ks], sem.at[a, c], zr.at[a, c], dev(z_=to))

    def feed(p, c, do_z):
        int_copy(p, c).start()
        y_copy(p, c).start()
        if p < 3:
            @pl.when((z > 0) & (z + p <= 3))
            def _():
                z_copy(z + p, c, z - 1, zd).start()

            @pl.when((z < 3) & (z - p >= 0))
            def _():
                z_copy(z - p, c, z + 1, zu).start()

    def arrive(p, c):
        int_copy(p, c).wait_recv()
        y_copy(p, c).wait_recv()
        if p < 3:
            @pl.when(z + p + 1 <= 3)
            def _():
                z_copy(z + p + 1, c, z - 1, zd).wait_recv()

            @pl.when(z - p - 1 >= 0)
            def _():
                z_copy(z - p - 1, c, z + 1, zu).wait_recv()

    def drain(p, c):
        int_copy(p, c).wait_send()
        y_copy(p, c).wait_send()
        if p < 3:
            @pl.when((z > 0) & (z + p <= 3))
            def _():
                z_copy(z + p, c, z - 1, zd).wait_send()

            @pl.when((z < 3) & (z - p >= 0))
            def _():
                z_copy(z - p, c, z + 1, zu).wait_send()

    def tick(t):
        arrive(t // CH, t % CH)
        if t:
            drain((t - 1) // CH, (t - 1) % CH)
        if t + AHEAD < 4 * CH:
            feed((t + AHEAD) // CH, (t + AHEAD) % CH, True)

    def fresh(p):
        if p == 4:
            return [(1, 3, 0, 512, 4), (1, 3, 512, 512, 5)]
        got = [(0, p, 0, 512 + 128 * p, p)]
        if p:
            got.append((1, p - 1, 0, 512 + 128 * p, p))
        return got

    def older(p):
        c0 = 512 + 128 * (p - 1)
        got = [(0, e, c0, 128, p) for e in range(min(p, 4))]
        return got + [(1, e, c0, 128, p) for e in range(p - 1)]

    def messages(p):
        return fresh(p) + older(p)

    def slot_of(side, e):
        return 4 * side + ords[e]

    def split(v):
        hi = v.astype(jnp.bfloat16)
        return hi, (v - hi.astype(jnp.float32)).astype(jnp.bfloat16)

    def prep_a(slot):
        t = abuf[slot].reshape(1600, 128).T
        hi, lo = split(t)
        at_h[slot] = hi
        at_l[slot] = lo

    def multiply(slot, c0, width):
        ah = at_h[slot]
        al = at_l[slot]
        n0 = c0
        while n0 < c0 + width:
            w = min(256, c0 + width - n0)
            b_h = bh[:, n0:n0 + w]
            b_l = bl[:, n0:n0 + w]
            acc = jnp.dot(ah, b_l, preferred_element_type=jnp.float32)
            acc += jnp.dot(al, b_h, preferred_element_type=jnp.float32)
            acc += jnp.dot(ah, b_h, preferred_element_type=jnp.float32)
            part[slot, :, :, n0:n0 + w] = acc.reshape(2, 64, w)
            n0 += w

    def s1_copy(m):
        side, e, c0, w, q = m
        slot = slot_of(side, e)
        cs = pl.ds(c0, w)
        return remote(
            part.at[slot, 1 - core, :, cs], r1.at[slot, :, cs],
            s1s.at[slot, q], s1r.at[slot, q], dev(core_=1 - core),
        )

    def part_rows(slot, i, cs):
        return part.at[slot, core, pl.ds(pl.multiple_of(16 * i, 16), 16), cs]

    def s2_copy(m, i, src_x, to):
        side, e, c0, w, q = m
        slot = slot_of(side, e)
        cs = pl.ds(c0, w)
        return remote(
            part_rows(slot, to, cs), r2.at[slot, i, :, cs],
            s2s.at[slot, i, q], s2r.at[slot, i, q], dev(x_=to),
        )

    def s3_copy(m, i):
        side, e, c0, w, q = m
        slot = slot_of(side, e)
        cs = pl.ds(c0, w)
        b = yp if side else y
        to = flip(b) if i == 0 else b
        k = 1 if i == 1 else 0
        return remote(
            part_rows(slot, x, cs), r3.at[ords[e], k, :, cs],
            s3s.at[slot, q], s3r.at[ords[e], k, q], dev(h_=to),
        )

    def fin_rows(i, cs):
        return fin.at[pl.ds(pl.multiple_of(16 * i, 16), 16), cs]

    def s4_own(side, e, src_x):
        slot = slot_of(side, e)
        cs = pl.ds(0, 512)
        return remote(
            part_rows(slot, x, cs), fin_rows(src_x, cs),
            s4s.at[ords[e], 0], s4r.at[src_x, 0], dev(x_=ords[e]),
        )

    def s4_far(m, src_x):
        side, e, c0, w, q = m
        slot = slot_of(side, e)
        w, c0 = c0 + w - max(c0, 512), max(c0, 512)
        return remote(
            part_rows(slot, x, pl.ds(c0, w)), fin_rows(src_x, pl.ds(c0 - 512, w)),
            s4s.at[ords[e], q], s4r.at[src_x, q], dev(x_=ords[e], y_=yq),
        )

    def stage2(p, pick=None):
        for m in messages(p) if pick is None else pick:
            side, e, c0, w, q = m
            slot = slot_of(side, e)
            s1_copy(m).wait_recv()
            part[slot, core, :, c0:c0 + w] = part[slot, core, :, c0:c0 + w] + r1[slot, :, c0:c0 + w]
            for i in range(3):
                s2_copy(m, i, x, lax.rem(x + 1 + i, 4)).start()

    def stage3(p, pick=None):
        for m in messages(p) if pick is None else pick:
            side, e, c0, w, q = m
            slot = slot_of(side, e)
            b = yp if side else y
            for i in range(3):
                s2_copy(m, i, x, lax.rem(x + 1 + i, 4)).wait_recv()
            rows = pl.ds(pl.multiple_of(16 * x, 16), 16)
            part[slot, core, rows, c0:c0 + w] = (
                part[slot, core, rows, c0:c0 + w] + r2[slot, 0, :, c0:c0 + w]
            ) + (r2[slot, 1, :, c0:c0 + w] + r2[slot, 2, :, c0:c0 + w])

            @pl.when(h == lax.rem(b + 2, 4))
            def _():
                s3_copy(m, 0).start()

            @pl.when(h == 3 - b)
            def _():
                s3_copy(m, 1).start()

    def stage3m(p, pick=None):
        for m in messages(p) if pick is None else pick:
            side, e, c0, w, q = m
            slot = slot_of(side, e)
            b = yp if side else y

            @pl.when(h == flip(b))
            def _():
                s3_copy(m, 0).wait_recv()
                rows = pl.ds(pl.multiple_of(16 * x, 16), 16)
                part[slot, core, rows, c0:c0 + w] = (
                    part[slot, core, rows, c0:c0 + w] + r3[ords[e], 0, :, c0:c0 + w]
                )
                s3_copy(m, 2).start()

    def stage4(p, pick=None):
        for m in messages(p) if pick is None else pick:
            side, e, c0, w, q = m
            slot = slot_of(side, e)
            b = yp if side else y
            a = ords[e]

            @pl.when(h == b)
            def _():
                s3_copy(m, 1).wait_recv()
                s3_copy(m, 2).wait_recv()
                rows = pl.ds(pl.multiple_of(16 * x, 16), 16)
                part[slot, core, rows, c0:c0 + w] = part[slot, core, rows, c0:c0 + w] + (
                    r3[a, 0, :, c0:c0 + w] + r3[a, 1, :, c0:c0 + w]
                )
                if c0 + w > 512:
                    s4_far(m, x).start()
                if c0 == 0:
                    @pl.when(a == x)
                    def _():
                        fin[rows, :] = part[slot, core, rows, 0:512]

                    @pl.when(a != x)
                    def _():
                        s4_own(side, e, x).start()

    def sent(p):
        for m in messages(p):
            s1_copy(m).wait_send()
            for i in range(3):
                s2_copy(m, i, x, lax.rem(x + 1 + i, 4)).wait_send()

    def compute_new(p):
        for m in fresh(p):
            side, e, c0, w, q = m
            slot = slot_of(side, e)
            if c0 == 0:
                prep_a(slot)
            multiply(slot, c0, w)
            s1_copy(m).start()

    def compute_old(ms):
        for m in ms:
            side, e, c0, w, q = m
            multiply(slot_of(side, e), c0, w)
            s1_copy(m).start()

    def prep_b_own():
        @pl.loop(0, 25)
        def _(k):
            hi, lo = split(bown[k])
            rows = pl.ds(pl.multiple_of(64 * k, 64), 64)
            bh[rows, 0:512] = hi
            bl[rows, 0:512] = lo

    def prep_b(q):
        @pl.loop(0, 25)
        def _(k):
            hi, lo = split(ib[q, k])
            rows = pl.ds(pl.multiple_of(64 * k, 64), 64)
            bh[rows, 512 + 128 * q:640 + 128 * q] = hi
            bl[rows, 512 + 128 * q:640 + 128 * q] = lo

    for t in range(AHEAD):
        feed(t // CH, t % CH, True)
    own_b.wait()
    tick(0)
    prep_b_own()
    tick(1)
    compute_new(0)
    tick(2)
    tick(3)
    stage2(0)
    tick(4)
    tick(5)
    prep_b(0)
    compute_new(1)
    tick(6)
    compute_old(older(1))
    tick(7)
    stage2(1)
    tick(8)
    tick(9)
    tick(10)
    prep_b(1)
    compute_new(2)
    tick(11)
    stage3(0)
    stage3(1)
    compute_old(older(2))
    tick(12)
    stage2(2)
    tick(13)
    stage3m(0)
    stage3m(1)
    sent(0)
    sent(1)
    tick(14)
    tick(15)
    prep_b(2)
    stage3(2)
    compute_new(3)
    tick(16)
    stage2(3, fresh(3))
    compute_old(older(3))
    tick(17)
    stage2(3, older(3))
    stage3m(2)
    tick(18)
    stage3(3, fresh(3))
    stage4(0)
    stage4(1)
    sent(2)
    tick(19)
    prep_b(3)
    compute_new(4)
    stage3(3, older(3))
    compute_old(older(4)[:3])
    stage2(4, fresh(4))
    stage3m(3)
    compute_old(older(4)[3:])
    stage4(2)
    stage3(4, fresh(4))
    stage2(4, older(4))
    sent(3)
    stage3m(4, fresh(4))
    stage3(4, older(4))
    stage4(3)
    stage4(4, fresh(4))
    stage3m(4, older(4))
    sent(4)
    stage4(4, older(4))

    for side in range(2):
        for e in range(4):
            @pl.when((ords[e] == x) & (h == (yp if side else y)))
            def _():
                for i in range(3):
                    s4_own(side, e, lax.rem(x + 1 + i, 4)).wait_recv()

            @pl.when((ords[e] == x) & (h == (3 - yq if side else yq)))
            def _():
                for p in range(5):
                    for m in messages(p):
                        if m[:2] == (side, e) and m[2] + m[3] > 512:
                            for i in range(4):
                                s4_far(m, i).wait_recv()
    out[...] = fin[...]

    drain(3, CH - 1)
    for p in range(5):
        for m in messages(p):
            side, e, c0, w, q = m
            b = yp if side else y

            @pl.when(h != b)
            def _():
                s3_copy(m, 1).wait_send()

            @pl.when(h == b)
            def _():
                if c0 + w > 512:
                    s4_far(m, x).wait_send()
                if c0 == 0:
                    @pl.when(ords[e] != x)
                    def _():
                        s4_own(side, e, x).wait_send()


def shards(amplitude, integral):
    f32, bf16 = jnp.float32, jnp.bfloat16
    dma = pltpu.SemaphoreType.DMA
    return pl.pallas_call(
        kernel,
        out_shape=jax.ShapeDtypeStruct((64, 512), f32),
        in_specs=[pl.BlockSpec(memory_space=pl.ANY)] * 2,
        out_specs=pl.BlockSpec(memory_space=pltpu.VMEM),
        scratch_shapes=[
            pltpu.VMEM((8, 25, 64, 128), f32),
            pltpu.VMEM((8, 128, 1600), bf16),
            pltpu.VMEM((8, 128, 1600), bf16),
            pltpu.VMEM((25, 64, 512), f32),
            pltpu.VMEM((1600, 1024), bf16),
            pltpu.VMEM((1600, 1024), bf16),
            pltpu.VMEM((4, 25, 64, 128), f32),
            pltpu.VMEM((8, 2, 64, 1024), f32),
            pltpu.VMEM((8, 64, 1024), f32),
            pltpu.VMEM((8, 3, 16, 1024), f32),
            pltpu.VMEM((4, 2, 16, 1024), f32),
            pltpu.VMEM((64, 512), f32),
            dma((2,)),
            dma((4, CH)), dma((4, CH)), dma((4, CH)),
            dma((4, CH)), dma((4, CH)),
            dma((4, CH)), dma((4, CH)),
            dma((8, 6)), dma((8, 6)),
            dma((8, 3, 6)), dma((8, 3, 6)),
            dma((8, 6)), dma((4, 2, 6)),
            dma((4, 6)), dma((4, 6)),
        ],
        compiler_params=pltpu.CompilerParams(
            collective_id=0, has_side_effects=True, vmem_limit_bytes=56 << 20
        ),
    )(amplitude, jnp.transpose(integral, (1, 0, 2)))


def solution(mesh):
    return jax.shard_map(
        shards,
        mesh=mesh,
        in_specs=(P("row", "depth", "col"), P("depth", None, "col")),
        out_specs=P(("row", "depth"), "col"),
        check_vma=False,
    )
```

```python
import functools

import jax
import jax.numpy as jnp
from jax import lax
from jax.experimental import pallas as pl
from jax.experimental.pallas import tpu as pltpu
from jax.sharding import PartitionSpec as P

MESH = pl.DeviceIdType.MESH
CH = 5
KC = 5
AHEAD = 5


def order(z, p):
    hi = z // 2
    zz = z + hi * (3 - 2 * z)
    base = p + zz * (1 - 2 * p) if p < 2 else p
    return base + hi * (3 - 2 * base)


def kernel(
    amp, integ, out,
    abuf, at_h, at_l, bown, bh, bl, ib, part, r1, r2, r3, fin,
    loc, ts, tr, zr, zd, zu, yr, ys, ir, js, s1s, s1r, s2s, s2r, s3s, s3r, s4s, s4r,
):
    x = lax.axis_index("row")
    col = lax.axis_index("col")
    dep = lax.axis_index("depth")
    z, y = col // 4, lax.rem(col, 4)
    h, core = dep // 2, lax.rem(dep, 2)
    yp = 3 - y

    def flip(v):
        return v + 1 - 2 * lax.rem(v, 2)

    yq = flip(y)
    ords = [order(z, p) for p in range(4)]

    def dev(x_=None, y_=None, z_=None, h_=None, core_=None):
        return (
            x if x_ is None else x_,
            (z if z_ is None else z_) * 4 + (y if y_ is None else y_),
            (h if h_ is None else h_) * 2 + (core if core_ is None else core_),
        )

    def remote(src, dst, ss, rs, to):
        return pltpu.make_async_remote_copy(
            src_ref=src, dst_ref=dst, send_sem=ss, recv_sem=rs,
            device_id=to, device_id_type=MESH,
        )

    own_a = pltpu.make_async_copy(amp, abuf.at[z], loc.at[0])
    own_b = pltpu.make_async_copy(integ.at[pl.ds(25 * x, 25)], bown, loc.at[1])
    own_a.start()
    own_b.start()

    barrier = pltpu.get_barrier_semaphore()

    def greet(to):
        pl.semaphore_signal(barrier, inc=1, device_id=to, device_id_type=MESH)

    greet(dev(y_=yp))
    greet(dev(y_=yq))
    greet(dev(core_=1 - core))
    for i in range(1, 4):
        greet(dev(x_=lax.rem(x + i, 4)))
    greet(dev(h_=lax.rem(h + 1, 4)))
    greet(dev(h_=lax.rem(h + 3, 4)))

    @pl.when(z > 0)
    def _():
        greet(dev(z_=z - 1))

    @pl.when(z < 3)
    def _():
        greet(dev(z_=z + 1))

    @pl.when((z > 0) & (z < 3))
    def _():
        pl.semaphore_wait(barrier, 10)

    @pl.when((z == 0) | (z == 3))
    def _():
        pl.semaphore_wait(barrier, 9)

    own_a.wait()

    def int_copy(p, c):
        return remote(
            integ.at[pl.ds(25 * x + KC * c, KC), :, pl.ds(128 * p, 128)],
            ib.at[p, pl.ds(KC * c, KC)],
            js.at[p, c], ir.at[p, c], dev(y_=yq),
        )

    def y_copy(p, c):
        a = ords[p]
        ks = pl.ds(KC * c, KC)
        return remote(abuf.at[a, ks], abuf.at[4 + a, ks], ys.at[a, c], yr.at[a, c], dev(y_=yp))

    def z_copy(a, c, to, sem):
        ks = pl.ds(KC * c, KC)
        return remote(abuf.at[a, ks], abuf.at[a, ks], sem.at[a, c], zr.at[a, c], dev(z_=to))

    def feed(p, c, do_z):
        int_copy(p, c).start()
        y_copy(p, c).start()
        if p < 3:
            @pl.when((z > 0) & (z + p <= 3))
            def _():
                z_copy(z + p, c, z - 1, zd).start()

            @pl.when((z < 3) & (z - p >= 0))
            def _():
                z_copy(z - p, c, z + 1, zu).start()

    def arrive(p, c):
        int_copy(p, c).wait_recv()
        y_copy(p, c).wait_recv()
        if p < 3:
            @pl.when(z + p + 1 <= 3)
            def _():
                z_copy(z + p + 1, c, z - 1, zd).wait_recv()

            @pl.when(z - p - 1 >= 0)
            def _():
                z_copy(z - p - 1, c, z + 1, zu).wait_recv()

    def drain(p, c):
        int_copy(p, c).wait_send()
        y_copy(p, c).wait_send()
        if p < 3:
            @pl.when((z > 0) & (z + p <= 3))
            def _():
                z_copy(z + p, c, z - 1, zd).wait_send()

            @pl.when((z < 3) & (z - p >= 0))
            def _():
                z_copy(z - p, c, z + 1, zu).wait_send()

    def tick(t):
        arrive(t // CH, t % CH)
        if t:
            drain((t - 1) // CH, (t - 1) % CH)
        if t + AHEAD < 4 * CH:
            feed((t + AHEAD) // CH, (t + AHEAD) % CH, True)

    def fresh(p):
        if p == 4:
            return [(1, 3, 0, 512, 4), (1, 3, 512, 384, 5)]
        got = [(0, p, 0, 512 + 128 * p, p)]
        if p:
            got.append((1, p - 1, 0, 512 + 128 * p, p))
        return got

    def older(p):
        if p == 4:
            return []
        c0 = 512 + 128 * (p - 1)
        got = [(0, e, c0, 128, p) for e in range(min(p, 4))]
        return got + [(1, e, c0, 128, p) for e in range(p - 1)]

    def messages(p):
        return fresh(p) + older(p)

    def slot_of(side, e):
        return 4 * side + ords[e]

    def split(v):
        hi = v.astype(jnp.bfloat16)
        return hi, (v - hi.astype(jnp.float32)).astype(jnp.bfloat16)

    def prep_a(slot):
        t = abuf[slot].reshape(1600, 128).T
        hi, lo = split(t)
        at_h[slot] = hi
        at_l[slot] = lo

    def multiply(slot, c0, width):
        ah = at_h[slot]
        al = at_l[slot]
        n0 = c0
        while n0 < c0 + width:
            w = min(256, c0 + width - n0)
            b_h = bh[:, n0:n0 + w]
            b_l = bl[:, n0:n0 + w]
            acc = jnp.dot(ah, b_l, preferred_element_type=jnp.float32)
            acc += jnp.dot(al, b_h, preferred_element_type=jnp.float32)
            acc += jnp.dot(ah, b_h, preferred_element_type=jnp.float32)
            part[slot, :, :, n0:n0 + w] = acc.reshape(2, 64, w)
            n0 += w

    def s1_copy(m):
        side, e, c0, w, q = m
        slot = slot_of(side, e)
        cs = pl.ds(c0, w)
        return remote(
            part.at[slot, 1 - core, :, cs], r1.at[slot, :, cs],
            s1s.at[slot, q], s1r.at[slot, q], dev(core_=1 - core),
        )

    def part_rows(slot, i, cs):
        return part.at[slot, core, pl.ds(pl.multiple_of(16 * i, 16), 16), cs]

    def s2_copy(m, i, src_x, to):
        side, e, c0, w, q = m
        slot = slot_of(side, e)
        cs = pl.ds(c0, w)
        return remote(
            part_rows(slot, to, cs), r2.at[slot, i, :, cs],
            s2s.at[slot, i, q], s2r.at[slot, i, q], dev(x_=to),
        )

    def s3_copy(m, i):
        side, e, c0, w, q = m
        slot = slot_of(side, e)
        cs = pl.ds(c0, w)
        b = yp if side else y
        to = flip(b) if i == 0 else b
        k = 1 if i == 1 else 0
        return remote(
            part_rows(slot, x, cs), r3.at[ords[e], k, :, cs],
            s3s.at[slot, q], s3r.at[ords[e], k, q], dev(h_=to),
        )

    def fin_rows(i, cs):
        return fin.at[pl.ds(pl.multiple_of(16 * i, 16), 16), cs]

    def s4_own(side, e, src_x):
        slot = slot_of(side, e)
        cs = pl.ds(0, 512)
        return remote(
            part_rows(slot, x, cs), fin_rows(src_x, cs),
            s4s.at[ords[e], 0], s4r.at[src_x, 0], dev(x_=ords[e]),
        )

    def s4_far(m, src_x):
        side, e, c0, w, q = m
        slot = slot_of(side, e)
        w, c0 = c0 + w - max(c0, 512), max(c0, 512)
        return remote(
            part_rows(slot, x, pl.ds(c0, w)), fin_rows(src_x, pl.ds(c0 - 512, w)),
            s4s.at[ords[e], q], s4r.at[src_x, q], dev(x_=ords[e], y_=yq),
        )

    def stage2(p, pick=None):
        for m in messages(p) if pick is None else pick:
            side, e, c0, w, q = m
            slot = slot_of(side, e)
            s1_copy(m).wait_recv()
            part[slot, core, :, c0:c0 + w] = part[slot, core, :, c0:c0 + w] + r1[slot, :, c0:c0 + w]
            for i in range(3):
                s2_copy(m, i, x, lax.rem(x + 1 + i, 4)).start()

    def stage3(p, pick=None):
        for m in messages(p) if pick is None else pick:
            side, e, c0, w, q = m
            slot = slot_of(side, e)
            b = yp if side else y
            for i in range(3):
                s2_copy(m, i, x, lax.rem(x + 1 + i, 4)).wait_recv()
            rows = pl.ds(pl.multiple_of(16 * x, 16), 16)
            part[slot, core, rows, c0:c0 + w] = (
                part[slot, core, rows, c0:c0 + w] + r2[slot, 0, :, c0:c0 + w]
            ) + (r2[slot, 1, :, c0:c0 + w] + r2[slot, 2, :, c0:c0 + w])

            @pl.when(h == lax.rem(b + 2, 4))
            def _():
                s3_copy(m, 0).start()

            @pl.when(h == 3 - b)
            def _():
                s3_copy(m, 1).start()

    def stage3m(p, pick=None):
        for m in messages(p) if pick is None else pick:
            side, e, c0, w, q = m
            slot = slot_of(side, e)
            b = yp if side else y

            @pl.when(h == flip(b))
            def _():
                s3_copy(m, 0).wait_recv()
                rows = pl.ds(pl.multiple_of(16 * x, 16), 16)
                part[slot, core, rows, c0:c0 + w] = (
                    part[slot, core, rows, c0:c0 + w] + r3[ords[e], 0, :, c0:c0 + w]
                )
                s3_copy(m, 2).start()

    def stage4(p, pick=None):
        for m in messages(p) if pick is None else pick:
            side, e, c0, w, q = m
            slot = slot_of(side, e)
            b = yp if side else y
            a = ords[e]

            @pl.when(h == b)
            def _():
                s3_copy(m, 1).wait_recv()
                s3_copy(m, 2).wait_recv()
                rows = pl.ds(pl.multiple_of(16 * x, 16), 16)
                part[slot, core, rows, c0:c0 + w] = part[slot, core, rows, c0:c0 + w] + (
                    r3[a, 0, :, c0:c0 + w] + r3[a, 1, :, c0:c0 + w]
                )
                if c0 + w > 512:
                    s4_far(m, x).start()
                if c0 == 0:
                    @pl.when(a == x)
                    def _():
                        fin[rows, :] = part[slot, core, rows, 0:512]

                    @pl.when(a != x)
                    def _():
                        s4_own(side, e, x).start()

    def sent(p):
        for m in messages(p):
            s1_copy(m).wait_send()
            for i in range(3):
                s2_copy(m, i, x, lax.rem(x + 1 + i, 4)).wait_send()

    def compute_new(p):
        for m in fresh(p):
            side, e, c0, w, q = m
            slot = slot_of(side, e)
            if c0 == 0:
                prep_a(slot)
            multiply(slot, c0, w)
            s1_copy(m).start()

    def compute_old(ms):
        for m in ms:
            side, e, c0, w, q = m
            multiply(slot_of(side, e), c0, w)
            s1_copy(m).start()

    def prep_b_own():
        @pl.loop(0, 25)
        def _(k):
            hi, lo = split(bown[k])
            rows = pl.ds(pl.multiple_of(64 * k, 64), 64)
            bh[rows, 0:512] = hi
            bl[rows, 0:512] = lo

    def prep_b(q):
        @pl.loop(0, 25)
        def _(k):
            hi, lo = split(ib[q, k])
            rows = pl.ds(pl.multiple_of(64 * k, 64), 64)
            bh[rows, 512 + 128 * q:640 + 128 * q] = hi
            bl[rows, 512 + 128 * q:640 + 128 * q] = lo

    LAST = 896
    TAIL = pl.ds(LAST, 128)
    PARTS = ((0, 10), (10, 20), (20, 25))

    def multiply_part(slot, c0, width, k0, k1):
        ah = at_h[slot, :, 64 * k0:64 * k1]
        al = at_l[slot, :, 64 * k0:64 * k1]
        n0 = c0
        while n0 < c0 + width:
            w = min(256, c0 + width - n0)
            b_h = bh[64 * k0:64 * k1, n0:n0 + w]
            b_l = bl[64 * k0:64 * k1, n0:n0 + w]
            acc = jnp.dot(ah, b_l, preferred_element_type=jnp.float32)
            acc += jnp.dot(al, b_h, preferred_element_type=jnp.float32)
            acc += jnp.dot(ah, b_h, preferred_element_type=jnp.float32)
            acc = acc.reshape(2, 64, w)
            if k0:
                acc += part[slot, :, :, n0:n0 + w]
            part[slot, :, :, n0:n0 + w] = acc
            n0 += w

    def last_part(i):
        k0, k1 = PARTS[i]
        slot = slot_of(1, 3)
        hi, lo = split(abuf[slot, k0:k1].reshape(64 * (k1 - k0), 128).T)
        at_h[slot, :, 64 * k0:64 * k1] = hi
        at_l[slot, :, 64 * k0:64 * k1] = lo
        hi, lo = split(ib[3, k0:k1].reshape(64 * (k1 - k0), 128))
        bh[64 * k0:64 * k1, LAST:1024] = hi
        bl[64 * k0:64 * k1, LAST:1024] = lo
        for m in fresh(4):
            multiply_part(slot, m[2], m[3], k0, k1)
            if i == 2:
                s1_copy(m).start()

        @pl.loop(0, 8)
        def _(t):
            multiply_part(t, LAST, 128, k0, k1)

        if i == 2:
            t1_copy().start()

    def t1_copy():
        return remote(
            part.at[:, 1 - core, :, TAIL], r1.at[:, :, TAIL], ts.at[0], tr.at[0], dev(core_=1 - core)
        )

    def t2_copy(i):
        to = lax.rem(x + 1 + i, 4)
        rows = pl.ds(pl.multiple_of(16 * to, 16), 16)
        return remote(
            part.at[:, core, rows, TAIL], r2.at[:, i, :, TAIL], ts.at[1 + i], tr.at[1 + i], dev(x_=to)
        )

    def t3_copy(side, i):
        b = yp if side else y
        to = flip(b) if i == 0 else b
        k = 1 if i == 1 else 0
        rows = pl.ds(pl.multiple_of(16 * x, 16), 16)
        return remote(
            part.at[pl.ds(4 * side, 4), core, rows, TAIL], r3.at[:, k, :, TAIL],
            ts.at[4 + side], tr.at[4 + k], dev(h_=to),
        )

    def tail2():
        t1_copy().wait_recv()
        for t in range(8):
            part[t, core, :, LAST:1024] = part[t, core, :, LAST:1024] + r1[t, :, LAST:1024]
        for i in range(3):
            t2_copy(i).start()

    def tail3():
        for i in range(3):
            t2_copy(i).wait_recv()
        rows = pl.ds(pl.multiple_of(16 * x, 16), 16)
        for t in range(8):
            part[t, core, rows, LAST:1024] = (
                part[t, core, rows, LAST:1024] + r2[t, 0, :, LAST:1024]
            ) + (r2[t, 1, :, LAST:1024] + r2[t, 2, :, LAST:1024])
        for side in range(2):
            b = yp if side else y

            @pl.when(h == lax.rem(b + 2, 4))
            def _():
                t3_copy(side, 0).start()

            @pl.when(h == 3 - b)
            def _():
                t3_copy(side, 1).start()

    def tail3m():
        rows = pl.ds(pl.multiple_of(16 * x, 16), 16)
        for side in range(2):
            @pl.when(h == flip(yp if side else y))
            def _():
                t3_copy(side, 0).wait_recv()
                for a in range(4):
                    t = 4 * side + a
                    part[t, core, rows, LAST:1024] = part[t, core, rows, LAST:1024] + r3[a, 0, :, LAST:1024]
                t3_copy(side, 2).start()

    def tail4():
        rows = pl.ds(pl.multiple_of(16 * x, 16), 16)
        for side in range(2):
            @pl.when(h == (yp if side else y))
            def _():
                t3_copy(side, 1).wait_recv()
                t3_copy(side, 2).wait_recv()
                for a in range(4):
                    t = 4 * side + a
                    part[t, core, rows, LAST:1024] = part[t, core, rows, LAST:1024] + (
                        r3[a, 0, :, LAST:1024] + r3[a, 1, :, LAST:1024]
                    )
                for e in range(4):
                    s4_far((side, e, LAST, 128, 4), x).start()

    for t in range(AHEAD):
        feed(t // CH, t % CH, True)
    own_b.wait()
    tick(0)
    prep_b_own()
    tick(1)
    compute_new(0)
    tick(2)
    tick(3)
    stage2(0)
    tick(4)
    tick(5)
    prep_b(0)
    compute_new(1)
    tick(6)
    compute_old(older(1))
    tick(7)
    stage2(1)
    tick(8)
    tick(9)
    tick(10)
    prep_b(1)
    compute_new(2)
    tick(11)
    stage3(0)
    stage3(1)
    compute_old(older(2))
    tick(12)
    stage2(2)
    tick(13)
    stage3m(0)
    stage3m(1)
    sent(0)
    sent(1)
    tick(14)
    tick(15)
    prep_b(2)
    stage3(2)
    compute_new(3)
    tick(16)
    stage2(3, fresh(3))
    compute_old(older(3))
    last_part(0)
    tick(17)
    stage2(3, older(3))
    stage3m(2)
    tick(18)
    stage3(3, fresh(3))
    last_part(1)
    stage4(0)
    stage4(1)
    sent(2)
    tick(19)
    last_part(2)
    stage3(3, older(3))
    stage2(4)
    stage3m(3, fresh(3))
    tail2()
    stage3(4)
    stage3m(3, older(3))
    stage4(2)
    tail3()
    sent(3)
    stage3m(4)
    stage4(3)
    tail3m()
    stage4(4)
    tail4()

    for side in range(2):
        for e in range(4):
            @pl.when((ords[e] == x) & (h == (yp if side else y)))
            def _():
                for i in range(3):
                    s4_own(side, e, lax.rem(x + 1 + i, 4)).wait_recv()

            @pl.when((ords[e] == x) & (h == (3 - yq if side else yq)))
            def _():
                for p in range(5):
                    for m in messages(p):
                        if m[:2] == (side, e) and m[2] + m[3] > 512:
                            for i in range(4):
                                s4_far(m, i).wait_recv()
                for i in range(4):
                    s4_far((side, e, LAST, 128, 4), i).wait_recv()
    out[...] = fin[...]

    drain(3, CH - 1)
    sent(4)
    t1_copy().wait_send()
    for i in range(3):
        t2_copy(i).wait_send()
    for side in range(2):
        b = yp if side else y

        @pl.when(h != b)
        def _():
            t3_copy(side, 1).wait_send()

        @pl.when(h == b)
        def _():
            for e in range(4):
                s4_far((side, e, LAST, 128, 4), x).wait_send()

    for p in range(5):
        for m in messages(p):
            side, e, c0, w, q = m
            b = yp if side else y

            @pl.when(h != b)
            def _():
                s3_copy(m, 1).wait_send()

            @pl.when(h == b)
            def _():
                if c0 + w > 512:
                    s4_far(m, x).wait_send()
                if c0 == 0:
                    @pl.when(ords[e] != x)
                    def _():
                        s4_own(side, e, x).wait_send()


def shards(amplitude, integral):
    f32, bf16 = jnp.float32, jnp.bfloat16
    dma = pltpu.SemaphoreType.DMA
    return pl.pallas_call(
        kernel,
        out_shape=jax.ShapeDtypeStruct((64, 512), f32),
        in_specs=[pl.BlockSpec(memory_space=pl.ANY)] * 2,
        out_specs=pl.BlockSpec(memory_space=pltpu.VMEM),
        scratch_shapes=[
            pltpu.VMEM((8, 25, 64, 128), f32),
            pltpu.VMEM((8, 128, 1600), bf16),
            pltpu.VMEM((8, 128, 1600), bf16),
            pltpu.VMEM((25, 64, 512), f32),
            pltpu.VMEM((1600, 1024), bf16),
            pltpu.VMEM((1600, 1024), bf16),
            pltpu.VMEM((4, 25, 64, 128), f32),
            pltpu.VMEM((8, 2, 64, 1024), f32),
            pltpu.VMEM((8, 64, 1024), f32),
            pltpu.VMEM((8, 3, 16, 1024), f32),
            pltpu.VMEM((4, 2, 16, 1024), f32),
            pltpu.VMEM((64, 512), f32),
            dma((2,)), dma((6,)), dma((6,)),
            dma((4, CH)), dma((4, CH)), dma((4, CH)),
            dma((4, CH)), dma((4, CH)),
            dma((4, CH)), dma((4, CH)),
            dma((8, 6)), dma((8, 6)),
            dma((8, 3, 6)), dma((8, 3, 6)),
            dma((8, 6)), dma((4, 2, 6)),
            dma((4, 6)), dma((4, 6)),
        ],
        compiler_params=pltpu.CompilerParams(
            collective_id=0, has_side_effects=True, vmem_limit_bytes=56 << 20
        ),
    )(amplitude, jnp.transpose(integral, (1, 0, 2)))


def solution(mesh):
    return jax.shard_map(
        shards,
        mesh=mesh,
        in_specs=(P("row", "depth", "col"), P("depth", None, "col")),
        out_specs=P(("row", "depth"), "col"),
        check_vma=False,
    )
```
